32 devices in a mesh: groups: 1, ep: 32 (over z, y, x, core).
Axes of the slice: x: 2, y: 2, z: 4, core: 2. Of those that a mesh axis runs over, the one named last changes fastest.
Arguments:
- tokens: bfloat16 [2, 256, 3584], P(None, ('groups', 'ep')), may hold values from -6 to 6
- expert_ids: int32 [2, 256, 8], P(None, ('groups', 'ep')), may hold values from 0 to 15, all different within a row; in each aligned block of 8 rows (0 to 7, 8 to 15, ..., all dimensions but the last counted through in order) at most 8 rows name the same one
- route_weight: float32 [2, 256, 8], P(None, ('groups', 'ep')), may hold values from 0.05 to 1
- gate_weight: bfloat16 [32, 3584, 512], P('ep'), may hold values from -0.09375 to 0.09375
- up_weight: bfloat16 [32, 3584, 512], P('ep'), may hold values from -0.09375 to 0.09375
- down_weight: bfloat16 [32, 512, 3584], P('ep'), may hold values from -0.1875 to 0.1875
Outputs:
- combined: bfloat16 [2, 256, 3584], P(None, ('groups', 'ep'))
The draws below stay inside these ranges and needn't reach their ends.
Inputs may be any that keep to these rules, and one draw needn't show every extreme that they name: `expert_ids`: each row names 8 different experts; within each step, the 8 rows of one device name any one expert at most 8 times.
All inputs are finite; a program needn't handle non-finite values.
Results may differ from the reference program's by a relative error of at most 0.0065.
Values may be sent and summed in bfloat16 or wider, within the bound.
No kernel may reach another device: no remote copies, remote signals or barrier semaphores. Data moves between devices by JAX's collectives and lax.ppermute only.
A program may use at most 64 MiB of HBM per device.

```python
import math
import jax
import jax.numpy as jnp
import numpy as np
from jax import lax

D_WIN = 3584
FF_WIN = 1024
TOP = 8
STEPS = 2
TOK_DEV = 8
EXPERTS = 16
CAP = 8
TOKENS = 256
N_EP = 32


def levels(rng, dims, pieces, least, top_value):
    factor_of, own = 1.0, jax.random.fold_in(rng, 6)
    for axis_at, shards_of in pieces:
        draws = jnp.exp(jax.random.uniform(jax.random.fold_in(own, axis_at), (shards_of,), jnp.float32, least / len(pieces), top_value / len(pieces)))
        factor_of = factor_of * jnp.repeat(draws, dims[axis_at] // shards_of).reshape([-1 if axis == axis_at else 1 for axis in range(len(dims))])
    return factor_of


def assign_block(stream_key, own, number, rows, number_of, top, reach, skew):
    ranking = jax.random.permutation(stream_key, number_of)
    heavy_load, usual = portions_of(number_of, rows * top, reach, skew, True), portions_of(number_of, rows * top, reach, skew, False)
    places = jnp.arange(number_of)

    def named(lengths, rotation):
        used = int((lengths > 0).sum())
        fixed = max(1, used // 4)
        shifted = fixed + (places - fixed + rotation * (used - fixed)) % max(1, number_of - fixed)
        return jnp.zeros((number_of,), jnp.int32).at[ranking[jnp.where(places < fixed, places, shifted)]].set(jnp.asarray(lengths, jnp.int32))

    lengths = jnp.where(number % 4 == 0, named(heavy_load, number // 4), named(usual, number - number // 4 - 1))
    mixed = jax.random.permutation(jax.random.fold_in(own, 3), number_of)
    source_of, sink = mixed[0:number_of // 2 * 2:2], mixed[1:number_of // 2 * 2:2]
    room = jnp.minimum(lengths[source_of] - 1, reach - lengths[sink]) // 2
    room = jnp.where((source_of == ranking[0]) | (sink == ranking[0]) | (lengths[sink] == 0), 0, jnp.maximum(room, 0))
    shifted = jax.random.randint(jax.random.fold_in(own, 4), (number_of // 2,), 0, 1 << 20) % (room + 1)
    lengths = lengths.at[source_of].add(-shifted).at[sink].add(shifted)
    members = jnp.searchsorted(jnp.cumsum(lengths), jnp.arange(rows * top), side="right").astype(jnp.int32)
    listing = members.reshape(top, rows).T
    listing = listing[jax.random.permutation(jax.random.fold_in(own, 1), rows)]
    rotation = jax.random.randint(jax.random.fold_in(own, 2), (rows, 1), 0, top)
    return jnp.take_along_axis(listing, (jnp.arange(top)[None, :] + rotation) % top, axis=1)


def portions_of(number_of, total, bound, skew, full):
    portions = [(1 << 20) // math.isqrt(grade ** skew) + 1 for grade in range(1, number_of + 1)]
    largest = bound if full else min(bound, max(-(-total // number_of), total * portions[0] // sum(portions)))
    least = 1 if total - largest >= number_of - 1 else 0
    holding, spare = [largest] + [least] * (number_of - 1), total - largest - least * (number_of - 1)
    while spare > 0:
        free = [i for i in range(1, number_of) if holding[i] < largest] or [i for i in range(1, number_of) if holding[i] < bound]
        mass, left = sum([portions[i] for i in free]), spare
        for i in free:
            extra = min(bound - holding[i], max(1, left * portions[i] // mass), spare)
            holding[i] = holding[i] + extra
            spare = spare - extra
    return np.array(holding)


def centred(key, shape, scale, reach, pieces=(), kind=jnp.bfloat16):
    values = jax.random.normal(key, shape, jnp.float32) * scale
    if len(pieces) > 0:
        values = levels(key, shape, pieces, -0.22, 0.18) * values
    return jnp.clip(values, min=-reach, max=reach).astype(kind)


def setup_inputs(seed: int = 0, part: int = 0) -> dict:
    splits = jax.random.split(jax.random.key(seed), 7)
    part_keys = jax.random.split(jax.random.fold_in(splits[6], part), 7)
    tokens = centred(part_keys[0], (STEPS, TOKENS, D_WIN), 1.0, 6.0, ((1, 32),))
    expert_ids_keys = jax.random.split(jax.random.fold_in(part_keys[1], 1), STEPS * TOKENS // TOK_DEV)
    expert_ids_turns = jax.random.permutation(jax.random.fold_in(part_keys[1], 3), STEPS * TOKENS // TOK_DEV)
    expert_ids = jax.vmap(lambda own, number: assign_block(jax.random.fold_in(part_keys[1], 2), own, number, TOK_DEV, EXPERTS, TOP, CAP, 2))(expert_ids_keys, expert_ids_turns).reshape((STEPS, TOKENS, TOP))
    route_weight = jnp.clip(jnp.exp(math.log(1.0) - 2.9957323 * jax.random.uniform(part_keys[2], (STEPS, TOKENS, TOP), jnp.float32) ** levels(part_keys[2], (STEPS, TOKENS, TOP), ((1, 32),), -0.2, 0.2)), 0.05, 1.0)
    gate_weight = centred(splits[3], (N_EP, D_WIN, FF_WIN // 2), D_WIN ** -0.5, 0.09375, ((0, 32),))
    up_weight = centred(splits[4], (N_EP, D_WIN, FF_WIN // 2), D_WIN ** -0.5, 0.09375, ((0, 32),))
    down_weight = centred(splits[5], (N_EP, FF_WIN // 2, D_WIN), FF_WIN ** -0.5, 0.1875, ((0, 32),))
    return {"tokens": tokens, "expert_ids": expert_ids, "route_weight": route_weight, "gate_weight": gate_weight, "up_weight": up_weight, "down_weight": down_weight}


def slot_layout(block_ids, expert_count, capacity):
    pairs = block_ids.reshape(-1).astype(jnp.int32)
    count = pairs.shape[0]
    one_hot = (pairs[:, None] == jnp.arange(expert_count, dtype=jnp.int32)[None, :]).astype(jnp.float32)
    order = jnp.arange(count, dtype=jnp.int32)
    earlier = (order[None, :] < order[:, None]).astype(jnp.float32)
    before = jnp.dot(earlier, one_hot, precision=lax.Precision.HIGHEST)
    slot_rank = jnp.sum(before * one_hot, axis=1).astype(jnp.int32)
    slot_index = pairs * capacity + slot_rank
    slot_source = jnp.full((expert_count * capacity,), count, jnp.int32).at[slot_index].set(order)
    return slot_index, slot_source


def reference(tokens, expert_ids, route_weight, gate_weight, up_weight, down_weight):
    half_units = FF_WIN // 2
    gates = gate_weight.reshape(EXPERTS, 2, D_WIN, half_units)
    ups = up_weight.reshape(EXPERTS, 2, D_WIN, half_units)
    downs = down_weight.reshape(EXPERTS, 2, half_units, D_WIN)
    outputs = []
    for step_index in range(STEPS):
        inputs = tokens[step_index]
        block_ids = expert_ids[step_index].reshape(N_EP, TOK_DEV, TOP)
        slot_index, slot_source = jax.vmap(lambda blk: slot_layout(blk, EXPERTS, CAP))(block_ids)
        local_row = (slot_source // TOP).astype(jnp.int32)
        unused = local_row == TOK_DEV
        offsets = (TOK_DEV * jnp.arange(N_EP, dtype=jnp.int32))[:, None]
        global_row = jnp.where(unused, jnp.int32(TOKENS), local_row + offsets).astype(jnp.int32)
        gathers = global_row.reshape(N_EP, EXPERTS, CAP).transpose(1, 0, 2).reshape(EXPERTS, N_EP * CAP)
        padded = jnp.concatenate([inputs, jnp.zeros((1, D_WIN), inputs.dtype)], axis=0)

        def apply_expert(operands):
            gate_m, up_m, down_m, rows_index = operands
            rows = padded[rows_index]
            total = jnp.zeros((rows.shape[0], D_WIN), jnp.float32)
            for half in range(2):
                gate = jnp.dot(rows, gate_m[half], preferred_element_type=jnp.float32)
                upper = jnp.dot(rows, up_m[half], preferred_element_type=jnp.float32)
                act = (jax.nn.silu(gate) * upper).astype(jnp.bfloat16)
                part = jnp.dot(act, down_m[half], preferred_element_type=jnp.float32).astype(jnp.bfloat16)
                total = total + part.astype(jnp.float32)
            return total.astype(jnp.bfloat16)

        results = lax.map(apply_expert, (gates, ups, downs, gathers))
        expert_of = slot_index // CAP
        slot_rank = slot_index % CAP
        sources = jnp.arange(N_EP, dtype=jnp.int32)[:, None]
        positions = (expert_of * (N_EP * CAP) + sources * CAP + slot_rank).astype(jnp.int32)
        picked = results.reshape(-1, D_WIN)[positions.reshape(-1)].reshape(TOKENS, TOP, D_WIN)
        summed = jnp.sum(route_weight[step_index][:, :, None] * picked.astype(jnp.float32), axis=1)
        outputs.append(summed.astype(jnp.bfloat16))
    return jnp.stack(outputs)
```

```python
import jax
import jax.numpy as jnp
from jax import lax
from jax.sharding import PartitionSpec as P

LANES = 128
PLANE = 4
SHARED_ROWS = 512


def exchange(block, count, distance):
    route = [(index, index ^ distance) for index in range(count)]
    return lax.ppermute(block, "ep", route)


def split_exact(values):
    pieces = []
    rest = values
    for _ in range(3):
        piece = lax.reduce_precision(rest, 8, 7)
        pieces.append(piece.astype(jnp.bfloat16))
        rest = rest - piece
    return pieces


def with_routes(tokens, expert_ids, route_weight):
    columns = [expert_ids.astype(jnp.bfloat16)] + split_exact(route_weight)
    extra = jnp.concatenate(columns, axis=1)
    extra = jnp.pad(extra, ((0, 0), (0, -extra.shape[1] % LANES)))
    return jnp.concatenate([tokens, extra], axis=1)


def gather_rows(block, count, layers):
    found = [block] + [exchange(block, count, 2 * PLANE * k) for k in range(1, layers)]
    column = jnp.concatenate(found, axis=0)
    found = [column] + [exchange(column, count, 2 * k) for k in range(1, PLANE)]
    mine = jnp.concatenate(found, axis=0)
    return jnp.concatenate([mine, exchange(mine, count, 1)], axis=0)


def add_rounded(terms):
    total = terms[0].astype(jnp.float32)
    for term in terms[1:]:
        total = total + term.astype(jnp.float32)
    return total.astype(jnp.bfloat16)


def reduce_rows(partial, count, layers):
    half = partial.shape[0] // 2
    total = add_rounded([partial[:half], exchange(partial[half:], count, 1)])
    rows = half // PLANE
    parts = [total[k * rows : (k + 1) * rows] for k in range(PLANE)]
    total = add_rounded([parts[0]] + [exchange(parts[k], count, 2 * k) for k in range(1, PLANE)])
    rows = rows // layers
    parts = [total[k * rows : (k + 1) * rows] for k in range(layers)]
    return add_rounded(
        [parts[0]] + [exchange(parts[k], count, 2 * PLANE * k) for k in range(1, layers)]
    )


def expert_half(rows, features, top, gate_m, up_m, down_m):
    expert = (lax.axis_index("ep") // 2).astype(jnp.float32)
    extra = rows[:, features : features + 4 * top].astype(jnp.float32)
    chosen = extra[:, :top] == expert
    weight = extra[:, top : 2 * top] + extra[:, 2 * top : 3 * top] + extra[:, 3 * top :]
    weight = jnp.sum(jnp.where(chosen, weight, 0.0), axis=1, keepdims=True)
    inputs = rows[:, :features]
    gate = jnp.dot(inputs, gate_m, preferred_element_type=jnp.float32)
    upper = jnp.dot(inputs, up_m, preferred_element_type=jnp.float32)
    act = (jax.nn.silu(gate) * upper * weight).astype(jnp.bfloat16)
    return jnp.dot(act, down_m, preferred_element_type=jnp.float32).astype(jnp.bfloat16)


def shards(tokens, expert_ids, route_weight, gate_weight, up_weight, down_weight):
    count = lax.axis_size("ep")
    layers = count // (2 * PLANE)
    steps, _, features = tokens.shape
    top = expert_ids.shape[2]
    outputs = []
    for step in range(steps):
        block = with_routes(tokens[step], expert_ids[step], route_weight[step])
        if outputs and count * block.shape[0] > SHARED_ROWS:
            block, outputs[-1] = lax.optimization_barrier((block, outputs[-1]))
        rows = gather_rows(block, count, layers)
        partial = expert_half(rows, features, top, gate_weight[0], up_weight[0], down_weight[0])
        outputs.append(reduce_rows(partial, count, layers))
    return jnp.stack(outputs)


def solution(mesh):
    in_specs = (
        P(None, ("groups", "ep"), None),
        P(None, ("groups", "ep"), None),
        P(None, ("groups", "ep"), None),
        P("ep", None, None),
        P("ep", None, None),
        P("ep", None, None),
    )
    out_specs = P(None, ("groups", "ep"), None)
    return jax.shard_map(shards, mesh=mesh, in_specs=in_specs, out_specs=out_specs, check_vma=False)
```

```python
import functools

import jax
import jax.numpy as jnp
from jax import lax
from jax.experimental import pallas as pl
from jax.experimental.pallas import tpu as pltpu
from jax.sharding import PartitionSpec as P

LANES = 128
CORE, X, Y, LAYER = 1, 2, 4, 8
CHUNK = 256
SHARED_ROWS = 512


def exchange(block, distance):
    count = lax.axis_size("ep")
    return lax.ppermute(block, "ep", [(index, index ^ distance) for index in range(count)])


def run(kernel, outs, *args, scratch=(), limit=None, flops=0):
    vmem = pl.BlockSpec(memory_space=pltpu.VMEM)
    smem = pl.BlockSpec(memory_space=pltpu.SMEM)
    return pl.pallas_call(
        kernel,
        out_shape=outs,
        in_specs=[smem if a.dtype == jnp.int32 and a.ndim == 1 else vmem for a in args],
        out_specs=[vmem] * len(outs),
        scratch_shapes=list(scratch),
        compiler_params=pltpu.CompilerParams(vmem_limit_bytes=limit),
        cost_estimate=pl.CostEstimate(flops=flops, transcendentals=0, bytes_accessed=1 << 20),
    )(*args)


def struct(rows, columns, dtype=jnp.bfloat16):
    return jax.ShapeDtypeStruct((rows, columns), dtype)


def f32(ref, lo=None, hi=None):
    return ref[lo:hi].astype(jnp.float32)


def route_kernel(experts, steps, tokens, ids, weight, *outs):
    rows, features = tokens.shape[1:]
    top = ids.shape[2]
    for step in range(steps):
        out = outs[step]
        out[:, :features] = tokens[step]
        width = out.shape[1] - features
        lane = lax.broadcasted_iota(jnp.int32, (rows, width), 1)
        named = lane % experts
        piece = lane // experts
        dense = jnp.zeros((rows, width), jnp.float32)
        for k in range(top):
            dense += jnp.where(named == ids[step, :, k : k + 1], weight[step, :, k : k + 1], 0.0)
        high = dense.astype(jnp.bfloat16).astype(jnp.float32)
        middle = (dense - high).astype(jnp.bfloat16).astype(jnp.float32)
        low = dense - high - middle
        parts = jnp.where(piece == 0, high, jnp.where(piece == 1, middle, low))
        out[:, features:] = jnp.where(piece < 3, parts, 0.0).astype(jnp.bfloat16)


def expert_kernel(experts, pieces, expert, *refs):
    sources = refs[:pieces]
    gate_m, up_m, down_m, own, other, rows_ref = refs[pieces:]
    features, units = gate_m.shape
    chunk = rows_ref.shape[0]
    half = own.shape[0]
    spans = []
    base = 0
    for source in sources:
        spans.append((source, base))
        base += source.shape[0]
    for start in range(0, base, chunk):
        for source, at in spans:
            lo, hi = max(at, start), min(at + source.shape[0], start + chunk)
            if lo < hi:
                rows_ref[lo - start : hi - start] = source[lo - at : hi - at]
        width = rows_ref.shape[1] - features
        lane = lax.broadcasted_iota(jnp.int32, (chunk, width), 1)
        mine = (lane % experts == expert[0]) & (lane < 3 * experts)
        extra = rows_ref[:, features:].astype(jnp.float32)
        weight = jnp.sum(jnp.where(mine, extra, 0.0), axis=1, keepdims=True)
        inputs = rows_ref[:, :features]
        gate = jnp.dot(inputs, gate_m[...], preferred_element_type=jnp.float32)
        upper = jnp.dot(inputs, up_m[...], preferred_element_type=jnp.float32)
        act = (gate / (1.0 + jnp.exp(-gate)) * upper).astype(jnp.bfloat16)
        part = jnp.dot(act, down_m[...], preferred_element_type=jnp.float32)
        part = (part * weight).astype(jnp.bfloat16)
        for target, at in ((own, 0), (other, half)):
            lo, hi = max(at, start), min(at + half, start + chunk)
            if lo < hi:
                target[lo - at : hi - at] = part[lo - start : hi - start]


def pair_kernel(own, got, send_x, send_y, keep, keep_x, keep_y):
    rows = keep.shape[0]
    h = rows // 2
    total = lambda lo, hi: f32(own, lo, hi) + f32(got, lo, hi)
    send_x[:h] = total(3 * rows, 3 * rows + h).astype(jnp.bfloat16)
    send_x[h:] = total(rows, rows + h).astype(jnp.bfloat16)
    send_y[:h] = total(3 * rows + h, 4 * rows).astype(jnp.bfloat16)
    send_y[h:] = total(2 * rows + h, 3 * rows).astype(jnp.bfloat16)
    keep[...] = total(0, rows)
    keep_x[...] = total(rows + h, 2 * rows)
    keep_y[...] = total(2 * rows, 2 * rows + h)


def plane_kernel(keep, keep_x, keep_y, got_x, got_y, send_x, send_y, kept):
    h = keep_x.shape[0]
    send_x[...] = (keep_x[...] + f32(got_y, 0, h)).astype(jnp.bfloat16)
    send_y[...] = (keep_y[...] + f32(got_x, 0, h)).astype(jnp.bfloat16)
    kept[:h] = keep[:h] + f32(got_x, h)
    kept[h:] = keep[h:] + f32(got_y, h)


def layer_kernel(kept, got_x, got_y, mine, *sends):
    h = got_x.shape[0]
    rows = mine.shape[0]
    for k in range(len(sends) + 1):
        at = k * rows
        got, base = (got_y, 0) if at < h else (got_x, h)
        total = kept[at : at + rows] + f32(got, at - base, at - base + rows)
        if k == 0:
            mine[...] = total
        else:
            sends[k - 1][...] = total.astype(jnp.bfloat16)


def final_kernel(steps, *refs):
    *parts, out = refs
    each = len(parts) // steps
    for step in range(steps):
        total = parts[step * each][...]
        for part in parts[step * each + 1 : (step + 1) * each]:
            total += part[...].astype(jnp.float32)
        out[step] = total.astype(jnp.bfloat16)


def gather_layers(block, layers):
    return jnp.concatenate([block] + [exchange(block, LAYER * k) for k in range(1, layers)])


def gather_plane(column):
    h = column.shape[0] // 2
    from_x, from_y = exchange(column, X), exchange(column, Y)
    across = [exchange(from_y[:h], X), exchange(from_x[h:], Y)]
    pieces = [column, from_x, from_y] + across
    return pieces + [exchange(piece, CORE) for piece in pieces]


def expert_half(pieces, experts, gate_m, up_m, down_m):
    rows = sum(piece.shape[0] for piece in pieces)
    features, units = gate_m.shape
    expert = (lax.axis_index("ep") // 2).astype(jnp.int32).reshape(1)
    chunk = min(CHUNK, rows)
    return run(
        functools.partial(expert_kernel, experts, len(pieces)),
        [struct(rows // 2, features)] * 2,
        expert,
        *pieces,
        gate_m,
        up_m,
        down_m,
        scratch=[pltpu.VMEM((chunk, pieces[0].shape[1]), jnp.bfloat16)],
        limit=48 << 20,
        flops=6 * rows * features * units,
    )


def reduce_plane(own, other, layers):
    rows = own.shape[0] // 4
    h = rows // 2
    features = own.shape[1]
    wide = functools.partial(struct, columns=features, dtype=jnp.float32)
    got = exchange(other, CORE)
    send_x, send_y, keep, keep_x, keep_y = run(
        pair_kernel,
        [struct(rows, features)] * 2 + [wide(rows), wide(h), wide(h)],
        own,
        got,
    )
    got_x, got_y = exchange(send_x, X), exchange(send_y, Y)
    send_x, send_y, kept = run(
        plane_kernel,
        [struct(h, features)] * 2 + [wide(rows)],
        keep,
        keep_x,
        keep_y,
        got_x,
        got_y,
    )
    got_x, got_y = exchange(send_x, X), exchange(send_y, Y)
    each = rows // layers
    return run(
        layer_kernel,
        [wide(each)] + [struct(each, features)] * (layers - 1),
        kept,
        got_x,
        got_y,
    )


def after(value, *others):
    return lax.optimization_barrier((value,) + others)[0]


def shards(tokens, expert_ids, route_weight, gate_weight, up_weight, down_weight):
    count = lax.axis_size("ep")
    experts = count // 2
    layers = count // LAYER
    steps, rows, features = tokens.shape
    matrices = gate_weight[0], up_weight[0], down_weight[0]
    width = features + -(-3 * experts // LANES) * LANES
    blocks = run(
        functools.partial(route_kernel, experts, steps),
        [struct(rows, width)] * steps,
        tokens,
        expert_ids,
        route_weight,
    )
    serial = count * rows > SHARED_ROWS
    parts = []
    previous = None
    for step in range(steps):
        block = blocks[step]
        if previous is not None:
            block = after(block, parts[0] if serial else previous)
        column = gather_layers(block, layers)
        previous = column
        pieces = gather_plane(column)
        own, other = expert_half(pieces, experts, *matrices)
        mine, *sends = reduce_plane(own, other, layers)
        parts += [mine] + [exchange(send, LAYER * (k + 1)) for k, send in enumerate(sends)]
    return run(
        functools.partial(final_kernel, steps),
        [jax.ShapeDtypeStruct((steps, rows, features), jnp.bfloat16)],
        *parts,
    )[0]


def solution(mesh):
    in_specs = (
        P(None, ("groups", "ep"), None),
        P(None, ("groups", "ep"), None),
        P(None, ("groups", "ep"), None),
        P("ep", None, None),
        P("ep", None, None),
        P("ep", None, None),
    )
    out_specs = P(None, ("groups", "ep"), None)
    return jax.shard_map(shards, mesh=mesh, in_specs=in_specs, out_specs=out_specs, check_vma=False)
```

```python
import functools

import jax
import jax.numpy as jnp
from jax import lax
from jax.experimental import pallas as pl
from jax.experimental.pallas import tpu as pltpu
from jax.sharding import PartitionSpec as P

LANES = 128
CORE, X, Y, LAYER = 1, 2, 4, 8
CHUNK = 256
SMALL_VMEM = 4 << 20

ROUTE_COST = 10**10

SHARED_ROWS = 512


def exchange(block, distance):
    count = lax.axis_size("ep")
    return lax.ppermute(block, "ep", [(index, index ^ distance) for index in range(count)])


def run(kernel, outs, *args, scratch=(), limit=SMALL_VMEM, flops=0, copied=0):
    vmem = pl.BlockSpec(memory_space=pltpu.VMEM)
    smem = pl.BlockSpec(memory_space=pltpu.SMEM)
    hbm = pl.BlockSpec(memory_space=pltpu.HBM)
    specs = [smem if a.dtype == jnp.int32 and a.ndim == 1 else vmem for a in args]
    specs[len(args) - copied :] = [hbm] * copied
    return pl.pallas_call(
        kernel,
        out_shape=outs,
        in_specs=specs,
        out_specs=[vmem] * len(outs),
        scratch_shapes=list(scratch),
        compiler_params=pltpu.CompilerParams(vmem_limit_bytes=limit),
        cost_estimate=pl.CostEstimate(flops=flops, transcendentals=0, bytes_accessed=1 << 20),
    )(*args)


def struct(rows, columns, dtype=jnp.bfloat16):
    return jax.ShapeDtypeStruct((rows, columns), dtype)


def f32(ref, lo=None, hi=None):
    return ref[lo:hi].astype(jnp.float32)


def route_kernel(experts, steps, expert, tokens, ids, weight, *refs):
    *outs, ids_ref, weight_ref, sems = refs
    rows, features = tokens.shape[1:]
    top = ids.shape[2]
    copies = [
        pltpu.make_async_copy(ids, ids_ref, sems.at[steps]),
        pltpu.make_async_copy(weight, weight_ref, sems.at[steps + 1]),
    ]
    for step in range(steps):
        target = outs[step].at[:, pl.ds(0, features)]
        copies.append(pltpu.make_async_copy(tokens.at[step], target, sems.at[step]))
    for copy in copies:
        copy.start()
    for copy in copies[:2]:
        copy.wait()
    for step in range(steps):
        out = outs[step]
        width = out.shape[1] - features
        lane = lax.broadcasted_iota(jnp.int32, (rows, width), 1)
        named = lane % experts
        piece = lane // experts
        dense = jnp.zeros((rows, width), jnp.float32)
        for k in range(top):
            chosen = named == ids_ref[step, :, k : k + 1]
            dense += jnp.where(chosen, weight_ref[step, :, k : k + 1], 0.0)
        high = dense.astype(jnp.bfloat16).astype(jnp.float32)
        middle = (dense - high).astype(jnp.bfloat16).astype(jnp.float32)
        low = dense - high - middle
        parts = jnp.where(piece == 0, high, jnp.where(piece == 1, middle, low))
        out[:, features:] = jnp.where(piece < 3, parts, 0.0).astype(jnp.bfloat16)
    for copy in copies[2:]:
        copy.wait()


def hold_kernel(*refs):
    refs[-1][...] = jnp.zeros_like(refs[-1])


def join_kernel(count, *refs):
    sources, out = refs[:count], refs[-1]
    at = 0
    for source in sources:
        out[at : at + source.shape[0]] = source[...]
        at += source.shape[0]


def expert_kernel(experts, pieces, expert, *refs):
    sources = refs[:pieces]
    gate_m, up_m, down_m, own, other, rows_ref = refs[pieces:]
    features, _ = gate_m.shape
    chunk = rows_ref.shape[0]
    half = own.shape[0]
    spans = []
    base = 0
    for source in sources:
        spans.append((source, base))
        base += source.shape[0]
    for start in range(0, base, chunk):
        for source, at in spans:
            lo, hi = max(at, start), min(at + source.shape[0], start + chunk)
            if lo < hi:
                rows_ref[lo - start : hi - start] = source[lo - at : hi - at]
        width = rows_ref.shape[1] - features
        lane = lax.broadcasted_iota(jnp.int32, (chunk, width), 1)
        mine = (lane % experts == expert[0]) & (lane < 3 * experts)
        extra = rows_ref[:, features:].astype(jnp.float32)
        weight = jnp.sum(jnp.where(mine, extra, 0.0), axis=1, keepdims=True)
        inputs = rows_ref[:, :features]
        gate = jnp.dot(inputs, gate_m[...], preferred_element_type=jnp.float32)
        upper = jnp.dot(inputs, up_m[...], preferred_element_type=jnp.float32)
        act = (gate / (1.0 + jnp.exp(-gate)) * upper).astype(jnp.bfloat16)
        part = jnp.dot(act, down_m[...], preferred_element_type=jnp.float32)
        part = (part * weight).astype(jnp.bfloat16)
        for target, at in ((own, 0), (other, half)):
            lo, hi = max(at, start), min(at + half, start + chunk)
            if lo < hi:
                target[lo - at : hi - at] = part[lo - start : hi - start]


def pair_kernel(own, got, send_x, send_y, keep, keep_x, keep_y):
    rows = keep.shape[0]
    h = rows // 2
    total = lambda lo, hi: f32(own, lo, hi) + f32(got, lo, hi)
    send_x[:h] = total(3 * rows, 3 * rows + h).astype(jnp.bfloat16)
    send_x[h:] = total(rows, rows + h).astype(jnp.bfloat16)
    send_y[:h] = total(3 * rows + h, 4 * rows).astype(jnp.bfloat16)
    send_y[h:] = total(2 * rows + h, 3 * rows).astype(jnp.bfloat16)
    keep[...] = total(0, rows)
    keep_x[...] = total(rows + h, 2 * rows)
    keep_y[...] = total(2 * rows, 2 * rows + h)


def plane_kernel(keep, keep_x, keep_y, got_x, got_y, send_x, send_y, kept):
    h = keep_x.shape[0]
    send_x[...] = (keep_x[...] + f32(got_y, 0, h)).astype(jnp.bfloat16)
    send_y[...] = (keep_y[...] + f32(got_x, 0, h)).astype(jnp.bfloat16)
    kept[:h] = keep[:h] + f32(got_x, h)
    kept[h:] = keep[h:] + f32(got_y, h)


def layer_kernel(kept, got_x, got_y, mine, *sends):
    h = got_x.shape[0]
    rows = mine.shape[0]
    for k in range(len(sends) + 1):
        at = k * rows
        got, base = (got_y, 0) if at < h else (got_x, h)
        total = kept[at : at + rows] + f32(got, at - base, at - base + rows)
        if k == 0:
            mine[...] = total
        else:
            sends[k - 1][...] = total.astype(jnp.bfloat16)


def final_kernel(steps, *refs):
    *parts, out = refs
    each = len(parts) // steps
    for step in range(steps):
        total = parts[step * each][...]
        for part in parts[step * each + 1 : (step + 1) * each]:
            total += part[...].astype(jnp.float32)
        out[step] = total.astype(jnp.bfloat16)


def join(kept, *pieces):
    rows = sum(piece.shape[0] for piece in pieces)
    out = [struct(rows, pieces[0].shape[1])]
    return run(functools.partial(join_kernel, len(pieces)), out, *pieces, *kept)[0]


def gather_layers(kept, block, layers):
    found = [exchange(block, LAYER * k) for k in range(1, layers)]
    return join(kept, block, *found)


def gather_plane(kept, column):
    h = column.shape[0] // 2
    from_x, from_y = exchange(column, X), exchange(column, Y)
    across_x = exchange(from_y[:h], X)
    across_y = exchange(from_x[h:], Y)
    first = exchange(join(kept, column, from_x, from_y), CORE)
    across = join(kept, across_x, across_y)
    second = exchange(across, CORE)
    return [column, from_x, from_y, across, first, second]


def expert_half(pieces, expert, experts, gate_m, up_m, down_m):
    rows = sum(piece.shape[0] for piece in pieces)
    features, _ = gate_m.shape
    chunk = min(CHUNK, rows)
    return run(
        functools.partial(expert_kernel, experts, len(pieces)),
        [struct(rows // 2, features)] * 2,
        expert,
        *pieces,
        gate_m,
        up_m,
        down_m,
        scratch=[pltpu.VMEM((chunk, pieces[0].shape[1]), jnp.bfloat16)],
        limit=SMALL_VMEM,
    )


def reduce_plane(own, other, layers):
    rows = own.shape[0] // 4
    h = rows // 2
    features = own.shape[1]
    wide = functools.partial(struct, columns=features, dtype=jnp.float32)
    got = exchange(other, CORE)
    send_x, send_y, keep, keep_x, keep_y = run(
        pair_kernel, [struct(rows, features)] * 2 + [wide(rows), wide(h), wide(h)], own, got
    )
    got_x, got_y = exchange(send_x, X), exchange(send_y, Y)
    send_x, send_y, kept = run(
        plane_kernel, [struct(h, features)] * 2 + [wide(rows)], keep, keep_x, keep_y, got_x, got_y
    )
    got_x, got_y = exchange(send_x, X), exchange(send_y, Y)
    each = rows // layers
    mine, *sends = run(
        layer_kernel, [wide(each)] + [struct(each, features)] * (layers - 1), kept, got_x, got_y
    )
    return [mine] + [exchange(send, LAYER * k) for k, send in enumerate(sends, start=1)]


def after(value, *others):
    return lax.optimization_barrier((value,) + others)[0]


def shards(tokens, expert_ids, route_weight, gate_weight, up_weight, down_weight):
    count = lax.axis_size("ep")
    experts = count // 2
    layers = count // LAYER
    steps, rows, features = tokens.shape
    matrices = gate_weight[0], up_weight[0], down_weight[0]
    width = features + -(-3 * experts // LANES) * LANES
    expert = lax.shift_right_logical(lax.axis_index("ep").astype(jnp.int32), 1).reshape(1)
    blocks = run(
        functools.partial(route_kernel, experts, steps),
        [struct(rows, width)] * steps,
        expert,
        tokens,
        expert_ids,
        route_weight,
        scratch=[
            pltpu.VMEM(expert_ids.shape, expert_ids.dtype),
            pltpu.VMEM(route_weight.shape, route_weight.dtype),
            pltpu.SemaphoreType.DMA((steps + 2,)),
        ],
        copied=3,
        flops=ROUTE_COST,
        limit=SMALL_VMEM,
    )
    hold = run(hold_kernel, [struct(8, 128)], *matrices)[0]
    matrices += (hold,)
    serial = count * rows > SHARED_ROWS
    parts = []
    for step in range(steps):
        block = blocks[step]
        if serial and parts:
            block = after(block, parts[0])
        column = gather_layers(matrices, block, layers)
        pieces = gather_plane(matrices, column)
        own, other = expert_half(pieces, expert, experts, *matrices[:3])
        parts += reduce_plane(own, other, layers)
    return run(
        functools.partial(final_kernel, steps),
        [jax.ShapeDtypeStruct((steps, rows, features), jnp.bfloat16)],
        *parts,
    )[0]


def solution(mesh):
    in_specs = (
        P(None, ("groups", "ep"), None),
        P(None, ("groups", "ep"), None),
        P(None, ("groups", "ep"), None),
        P("ep", None, None),
        P("ep", None, None),
        P("ep", None, None),
    )
    out_specs = P(None, ("groups", "ep"), None)
    return jax.shard_map(
        shards, mesh=mesh, in_specs=in_specs, out_specs=out_specs, check_vma=False
    )
```
